32 devices in a mesh: term: 8 (over y, x, core), rep: 4 (over z).
Axes of the slice: x: 2, y: 2, z: 4, core: 2. Of those that a mesh axis runs over, the one named last changes fastest.
Arguments:
- panel_values: float32 [16, 8, 128, 128], P('rep', 'term'), may hold values from 0.01 to 0.3
- panel_ids: int32 [16, 8], P('rep', 'term'), may hold values from 0 to 1953, as said below
- block_rows: int32 [1792], P('term'), may hold values from 0 to 1953, as said below
- block_cols: int32 [1792], P('term'), may hold values from 0 to 1953, as said below
Outputs:
- blocks_out: float32 [1792, 128, 128], P(('term', 'rep'))
The draws below stay inside these ranges and needn't reach their ends.
Inputs may be any that keep to these rules, and one draw needn't show every extreme that they name: `panel_ids`: the 8 tile ids of one panel are distinct. For every output block b, some panel lists both block_rows[b] and block_cols[b]. For every output block b, some panel lists both block_rows[b] and block_cols[b].
All inputs are finite; a program needn't handle non-finite values.
Results may differ from the reference program's by a relative error of at most 0.0003.
Values sent between devices are 32-bit elements; how exact they have to be, the bound alone decides.
A program may use at most 192 MiB of HBM per device.

```python
import math
import jax
import jax.numpy as jnp
from jax import lax

VT = 1954
TILE = 128
PASS = 128
PANELS = 16
NZT = 8
HOTN = 16
HOT_PANEL = 6
NB = 1792


def pools(key):
    shuffled = (jax.random.permutation(jax.random.fold_in(key, 11), VT - 2) + 1).astype(jnp.int32)
    hot_pool = jnp.concatenate([jnp.array([0, VT - 1], jnp.int32), shuffled[:HOTN - 2]])
    cold_pool = shuffled[HOTN - 2:]
    return (hot_pool, cold_pool)


def pick_panel(key, panel, hot_pool, cold_pool):
    base = jax.random.fold_in(key, 1000 + panel)
    scores = jax.random.permutation(jax.random.fold_in(base, 1), HOTN).astype(jnp.int32)
    positions = jnp.arange(HOTN, dtype=jnp.int32)
    scores = jnp.where((panel == 0) & (positions < 2), positions - 2, scores)
    hot_pick = jnp.argsort(scores)[:HOT_PANEL]
    cold_pick = jax.random.permutation(jax.random.fold_in(base, 2), VT - HOTN)[:NZT - HOT_PANEL]
    chosen = jnp.concatenate([hot_pool[hot_pick], cold_pool[cold_pick]])
    mixing = jax.random.permutation(jax.random.fold_in(base, 3), NZT)
    return chosen[mixing]


def draw_panel_ids(key, part):
    hot_pool, cold_pool = pools(key)
    panels = jnp.arange(PANELS, dtype=jnp.int32)
    return jax.vmap(lambda panel: pick_panel(key, panel, hot_pool, cold_pool))(panels).astype(jnp.int32)


def block_pairs(key):
    table = draw_panel_ids(key, 0).reshape(PANELS * NZT)
    base = jax.random.fold_in(key, 21)
    chosen = jax.random.randint(jax.random.fold_in(base, 1), (NB,), 0, PANELS).astype(jnp.int32)
    slot_row = jax.random.randint(jax.random.fold_in(base, 2), (NB,), 0, NZT).astype(jnp.int32)
    slot_col = jax.random.randint(jax.random.fold_in(base, 3), (NB,), 0, NZT).astype(jnp.int32)
    rows = table[chosen * NZT + slot_row]
    cols = table[chosen * NZT + slot_col]
    rows = rows.at[0].set(0).at[1].set(VT - 1)
    cols = cols.at[0].set(VT - 1).at[1].set(0)
    return (rows.astype(jnp.int32), cols.astype(jnp.int32))


def draw_block_rows(key, part):
    return block_pairs(key)[0]


def draw_block_cols(key, part):
    return block_pairs(key)[1]


def block_scale(stream_key, extent, pieces, smallest, largest):
    factor_of, own = 1.0, jax.random.fold_in(stream_key, 6)
    for dim, parts in pieces:
        heights = jnp.exp(jax.random.uniform(jax.random.fold_in(own, dim), (parts,), jnp.float32, smallest / len(pieces), largest / len(pieces)))
        factor_of = factor_of * jnp.repeat(heights, extent[dim] // parts).reshape([-1 if axis == dim else 1 for axis in range(len(extent))])
    return factor_of


def setup_inputs(seed: int = 0) -> dict:
    arg_keys = jax.random.split(jax.random.key(seed), 5)
    panel_values = jnp.clip(jnp.exp(math.log(0.3) - 3.4011974 * jax.random.uniform(arg_keys[0], (PANELS, NZT, PASS, TILE), jnp.float32) ** block_scale(arg_keys[0], (PANELS, NZT, PASS, TILE), ((0, 4), (1, 8)), -0.2, 0.2)), 0.01, 0.3)
    panel_ids = draw_panel_ids(jax.random.fold_in(arg_keys[4], 71), 0)
    block_rows = draw_block_rows(jax.random.fold_in(arg_keys[4], 71), 0)
    block_cols = draw_block_cols(jax.random.fold_in(arg_keys[4], 71), 0)
    return {"panel_values": panel_values, "panel_ids": panel_ids, "block_rows": block_rows, "block_cols": block_cols}


def block_terms(tile_values, tile_ids, row_ids, col_ids):
    match_row = tile_ids[None, :] == row_ids[:, None]
    match_col = tile_ids[None, :] == col_ids[:, None]
    slot_row = jnp.argmax(match_row, axis=1).astype(jnp.int32)
    slot_col = jnp.argmax(match_col, axis=1).astype(jnp.int32)
    present = jnp.any(match_row, axis=1) & jnp.any(match_col, axis=1)
    left_tile = jnp.take(tile_values, slot_row, axis=0)
    right_tile = jnp.take(tile_values, slot_col, axis=0)
    product = jnp.einsum("gpi,gpj->gij", left_tile, right_tile, precision=lax.Precision.HIGHEST)
    return jnp.where(present[:, None, None], product, jnp.float32(0.0))


def reference(panel_values, panel_ids, block_rows, block_cols):
    width = math.gcd(NB, 256)
    rows_grouped = block_rows.reshape(NB // width, width)
    cols_grouped = block_cols.reshape(NB // width, width)

    def add_panel(total, panel):
        tile_values, tile_ids = panel

        def one_group(pair):
            return block_terms(tile_values, tile_ids, pair[0], pair[1])

        terms = lax.map(one_group, (rows_grouped, cols_grouped))
        return total + terms.reshape(NB, TILE, TILE), None

    start = jnp.zeros((NB, TILE, TILE), jnp.float32)
    total, _ = lax.scan(add_panel, start, (panel_values, panel_ids))
    return total
```

```python
import functools

import jax
import jax.numpy as jnp
from jax import lax
from jax.experimental import pallas as pl
from jax.experimental.pallas import tpu as pltpu
from jax.sharding import PartitionSpec as P

MESH = pl.DeviceIdType.MESH
CORES = 2
SIDE = 2
ID_ROWS = 8
UNROLL = 4


def gather_kernel(depth, shard_ref, all_ref, own_sem, send_sem, recv_sem):
    term = lax.axis_index("term")
    z = lax.axis_index("rep")
    core = term % CORES
    x = (term // CORES) % SIDE
    y = term // (CORES * SIDE)
    terms = CORES * SIDE * SIDE
    term_x = (y * SIDE + 1 - x) * CORES + core
    term_y = ((1 - y) * SIDE + x) * CORES + core
    term_c = (y * SIDE + x) * CORES + 1 - core
    UP, DOWN, X, Y, C = range(5)
    target = {UP: (term, z + 1), DOWN: (term, z - 1), X: (term_x, z), Y: (term_y, z), C: (term_c, z)}

    barrier = pltpu.get_barrier_semaphore()

    def greet(way):
        pl.semaphore_signal(barrier, inc=1, device_id=target[way], device_id_type=MESH)

    for way in (X, Y, C):
        greet(way)
    pl.when(z < depth - 1)(lambda: greet(UP))
    pl.when(z > 0)(lambda: greet(DOWN))
    pl.semaphore_wait(barrier, 3 + (z < depth - 1).astype(jnp.int32) + (z > 0).astype(jnp.int32))

    def slot_of(at_x, at_y, at_z, at_core):
        return at_z * terms + (at_y * SIDE + at_x) * CORES + at_core

    def copy(way, place, src=None):
        at_x, at_y, at_z = place
        slot = slot_of(at_x, at_y, at_z, core)
        return pltpu.make_async_remote_copy(
            src_ref=all_ref.at[slot] if src is None else src,
            dst_ref=all_ref.at[slot],
            send_sem=send_sem.at[way, (at_z * SIDE + at_y) * SIDE + at_x],
            recv_sem=recv_sem.at[slot],
            device_id=target[way],
            device_id_type=MESH,
        )

    sent = []

    def send(way, place, valid=None, src=None):
        sent.append((way, place, valid, src))
        if valid is None:
            copy(way, place, src).start()
        else:
            pl.when(valid)(lambda: copy(way, place, src).start())

    def arrived(at_x, at_y, at_z, at_core, valid=None):
        slot = slot_of(at_x, at_y, at_z, at_core)

        def take():
            pltpu.make_async_remote_copy(
                src_ref=all_ref.at[slot], dst_ref=all_ref.at[slot], send_sem=send_sem.at[0, 0],
                recv_sem=recv_sem.at[slot], device_id=target[C], device_id_type=MESH,
            ).wait_recv()

        if valid is None:
            take()
        else:
            pl.when(valid)(take)

    def both(a, b):
        return b if a is None else a if b is None else a & b

    def spread(at_z, valid, src=None):
        for way in (X, Y, C):
            send(way, (x, y, at_z), valid, src)

    def cross(at_z, valid):
        even = at_z % 2 == 0
        arrived(1 - x, y, at_z, core, valid)
        send(Y, (1 - x, y, at_z), both(valid, even))
        send(C, (1 - x, y, at_z), valid)
        arrived(x, 1 - y, at_z, core, valid)
        send(X, (x, 1 - y, at_z), both(valid, at_z % 2 == 1))
        send(C, (x, 1 - y, at_z), valid)

    def corner(at_z, valid):
        arrived(1 - x, 1 - y, at_z, core, valid)
        send(C, (1 - x, 1 - y, at_z), valid)

    own = pltpu.make_async_copy(shard_ref, all_ref.at[slot_of(x, y, z, core)], own_sem)
    own.start()
    send(UP, (x, y, z), z < depth - 1, shard_ref)
    send(DOWN, (x, y, z), z > 0, shard_ref)
    spread(z, None, shard_ref)

    def level(far):
        if far == 0:
            return [(z, None)]
        return [(z - far, z >= far), (z + far, z + far < depth)]

    for far in range(1, depth + 2):
        if far < depth:
            low, low_ok = level(far)[0]
            high, high_ok = level(far)[1]
            arrived(x, y, low, core, low_ok)
            send(UP, (x, y, low), low_ok & (z < depth - 1))
            spread(low, low_ok)
            arrived(x, y, high, core, high_ok)
            send(DOWN, (x, y, high), high_ok & (z > 0))
            spread(high, high_ok)
        if far - 1 < depth:
            for at_z, valid in level(far - 1):
                cross(at_z, valid)
        if far >= 2:
            for at_z, valid in level(far - 2):
                corner(at_z, valid)

    for at_z in range(depth):
        for at_y in range(SIDE):
            for at_x in range(SIDE):
                arrived(at_x, at_y, at_z, 1 - core)
    own.wait()
    for way, place, valid, src in sent:
        if valid is None:
            copy(way, place, src).wait_send()
        else:
            pl.when(valid)(lambda: copy(way, place, src).wait_send())


def gather_by_hand(shard, depth):
    terms = CORES * SIDE * SIDE
    return pl.pallas_call(
        functools.partial(gather_kernel, depth),
        out_shape=jax.ShapeDtypeStruct((depth * terms,) + shard.shape, shard.dtype),
        in_specs=[pl.BlockSpec(memory_space=pl.ANY)],
        out_specs=pl.BlockSpec(memory_space=pl.ANY),
        scratch_shapes=[
            pltpu.SemaphoreType.DMA,
            pltpu.SemaphoreType.DMA((5, depth * SIDE * SIDE)),
            pltpu.SemaphoreType.DMA((depth * terms,)),
        ],
        compiler_params=pltpu.CompilerParams(collective_id=0, has_side_effects=True),
    )(shard)


def product_kernel(slots, base, count_ref, list_ref, tiles_ref, out_ref, left_ref, right_ref):
    panel = pl.program_id(0)

    @pl.when(panel == 0)
    def _():
        def clear(b, _):
            out_ref[b] = jnp.zeros(out_ref.shape[1:], jnp.float32)
            return 0

        lax.fori_loop(0, out_ref.shape[0], clear, 0)

    size = tiles_ref.shape[-1]

    def split(value):
        high = value.astype(jnp.bfloat16)
        return high, (value - high.astype(jnp.float32)).astype(jnp.bfloat16)

    def prepare(s):
        value = tiles_ref[0, s]
        high, low = split(value)
        right_ref[s, :size] = high
        right_ref[s, size : 2 * size] = high
        right_ref[s, 2 * size :] = low
        high, low = split(value.T)
        left_ref[s, :, :size] = high
        left_ref[s, :, size : 2 * size] = low
        left_ref[s, :, 2 * size :] = high

    if slots <= 8:
        for s in range(slots):
            prepare(s)
    else:
        pl.loop(0, slots)(prepare)

    def entries(first, width):
        picked = []
        for k in range(width):
            code = list_ref[panel * base + first + k]
            pair = code % (slots * slots)
            picked.append((code // (slots * slots), pair // slots, pair % slots))
        sums = [
            out_ref[b] + jnp.dot(left_ref[r], right_ref[c], preferred_element_type=jnp.float32)
            for b, r, c in picked
        ]
        for (b, _, _), value in zip(picked, sums):
            out_ref[b] = value

    count = count_ref[panel]
    groups = count // UNROLL
    pl.loop(0, groups)(lambda i: entries(i * UNROLL, UNROLL))
    pl.loop(groups * UNROLL, count)(lambda i: entries(i, 1))


def products(tiles, slots, panels_each, counts, entries, blocks):
    groups, size = tiles.shape[0], tiles.shape[3]
    return pl.pallas_call(
        functools.partial(product_kernel, slots, entries.shape[1]),
        out_shape=jax.ShapeDtypeStruct((blocks, size, size), jnp.float32),
        grid_spec=pltpu.PrefetchScalarGridSpec(
            num_scalar_prefetch=2,
            grid=(groups * panels_each,),
            in_specs=[
                pl.BlockSpec(
                    (1, slots, size, size), lambda p, *_: (p // panels_each, 0, p % panels_each, 0)
                )
            ],
            out_specs=pl.BlockSpec((blocks, size, size), lambda p, *_: (0, 0, 0)),
            scratch_shapes=[
                pltpu.VMEM((slots, size, 3 * size), jnp.bfloat16),
                pltpu.VMEM((slots, 3 * size, size), jnp.bfloat16),
            ],
        ),
        compiler_params=pltpu.CompilerParams(
            dimension_semantics=("arbitrary",), vmem_limit_bytes=56 * 1024 * 1024
        ),
    )(counts, entries.reshape(-1), tiles)


def block_list(ids, rows, cols):
    slots, blocks = ids.shape[1], rows.shape[0]
    order = jnp.arange(slots, dtype=jnp.int32)[None, :, None]
    match_row = ids[:, :, None] == rows[None, None, :]
    match_col = ids[:, :, None] == cols[None, None, :]
    slot_row = jnp.sum(jnp.where(match_row, order, 0), axis=1)
    slot_col = jnp.sum(jnp.where(match_col, order, 0), axis=1)
    present = jnp.any(match_row, axis=1) & jnp.any(match_col, axis=1)
    number = jnp.arange(blocks, dtype=jnp.int32)
    code = (number[None, :] * slots + slot_row) * slots + slot_col
    ahead = jnp.sum(
        jnp.where(present[:, None, :] & (number[None, None, :] < number[None, :, None]), 1, 0), axis=2
    )
    chosen = present[:, None, :] & (ahead[:, None, :] == number[None, :, None])
    entries = jnp.sum(jnp.where(chosen, code[:, None, :], 0), axis=2)
    counts = jnp.sum(present.astype(jnp.int32), axis=1)
    return counts.astype(jnp.int32), entries.astype(jnp.int32)


def solution(mesh):
    depth, terms = mesh.shape["rep"], mesh.shape["term"]
    by_hand = terms == CORES * SIDE * SIDE

    def local(panel_values, panel_ids, block_rows, block_cols):
        panels_each, own_slots, passages, size = panel_values.shape
        blocks = block_rows.shape[0] // depth
        slots = terms * own_slots
        first = lax.axis_index("rep") * blocks
        rows = lax.dynamic_slice_in_dim(block_rows, first, blocks)
        cols = lax.dynamic_slice_in_dim(block_cols, first, blocks)
        if by_hand and own_slots == 1:
            ids = jnp.broadcast_to(panel_ids.reshape(-1).astype(jnp.float32)[:, None], (panels_each, size))
            ids = jnp.pad(ids, ((0, -panels_each % ID_ROWS), (0, 0)))
            shard = jnp.concatenate([panel_values.reshape(panels_each * passages, size), ids], axis=0)
            tiles = gather_by_hand(shard, depth).reshape(depth, terms, -1, size)
            start = panels_each * passages
            ids = tiles[:, :, start : start + panels_each, 0].astype(jnp.int32)
        else:
            shard = jnp.swapaxes(panel_values, 0, 1).reshape(own_slots, panels_each * passages, size)
            tiles = lax.all_gather(shard, ("rep", "term"), axis=0, tiled=True)
            tiles = tiles.reshape(depth, slots, panels_each * passages, size)
            ids = lax.all_gather(panel_ids.T, ("rep", "term"), axis=0, tiled=True)
            ids = ids.reshape(depth, slots, panels_each)
        ids = jnp.swapaxes(ids, 1, 2).reshape(depth * panels_each, slots)
        counts, entries = block_list(ids, rows, cols)
        return products(tiles, slots, panels_each, counts, entries, blocks)

    placed = (P("rep", "term", None, None), P("rep", "term"), P("term"), P("term"))
    return jax.shard_map(
        local, mesh=mesh, in_specs=placed, out_specs=P(("term", "rep"), None, None), check_vma=False
    )
```

```python
import functools

import jax
import jax.numpy as jnp
from jax import lax
from jax.experimental import pallas as pl
from jax.experimental.pallas import tpu as pltpu
from jax.sharding import PartitionSpec as P

MESH = pl.DeviceIdType.MESH
CORES = 2
SIDE = 2
ROWS = 8
LANES = 128
PARTS = 2
CROSS_LAG = 1
CORNER_LAG = 2
UNROLL = 6


def gather_kernel(depth, blocks, meta_ref, shard_ref, all_ref, list_ref, ids_ref, own_sem, send_sem, recv_sem):
    term = lax.axis_index("term")
    z = lax.axis_index("rep")
    core = term % CORES
    x = (term // CORES) % SIDE
    y = term // (CORES * SIDE)
    terms = CORES * SIDE * SIDE
    term_x = (y * SIDE + 1 - x) * CORES + core
    term_y = ((1 - y) * SIDE + x) * CORES + core
    term_c = (y * SIDE + x) * CORES + 1 - core
    UP, DOWN, X, Y, C = range(5)
    target = {UP: (term, z + 1), DOWN: (term, z - 1), X: (term_x, z), Y: (term_y, z), C: (term_c, z)}

    barrier = pltpu.get_barrier_semaphore()

    def greet(way):
        pl.semaphore_signal(barrier, inc=1, device_id=target[way], device_id_type=MESH)

    for way in (X, Y, C):
        greet(way)
    pl.when(z < depth - 1)(lambda: greet(UP))
    pl.when(z > 0)(lambda: greet(DOWN))
    own_slot = z * terms + term
    own = pltpu.make_async_copy(shard_ref, all_ref.at[own_slot], own_sem)
    own.start()
    ids_ref[own_slot] = meta_ref[:ROWS]
    pl.semaphore_wait(barrier, 3 + (z < depth - 1).astype(jnp.int32) + (z > 0).astype(jnp.int32))

    cut = shard_ref.shape[0] // PARTS

    def slot_of(at_x, at_y, at_z, at_core):
        return at_z * terms + (at_y * SIDE + at_x) * CORES + at_core

    def part_of(slot, part):
        return ids_ref.at[slot] if part == 0 else all_ref.at[slot, pl.ds((part - 1) * cut, cut)]

    def copy(way, place, part, first):
        at_x, at_y, at_z = place
        slot = slot_of(at_x, at_y, at_z, core)
        source = part_of(slot, part)
        if first:
            source = meta_ref.at[pl.ds(0, ROWS)] if part == 0 else shard_ref.at[pl.ds((part - 1) * cut, cut)]
        return pltpu.make_async_remote_copy(
            src_ref=source,
            dst_ref=part_of(slot, part),
            send_sem=send_sem.at[part, way, (at_z * SIDE + at_y) * SIDE + at_x],
            recv_sem=recv_sem.at[part, slot],
            device_id=target[way],
            device_id_type=MESH,
        )

    sent = []

    def when(valid, act):
        if valid is None:
            act()
        else:
            pl.when(valid)(act)

    def send(way, place, part, valid=None, first=False):
        sent.append((way, place, part, valid, first))
        when(valid, lambda: copy(way, place, part, first).start())

    def arrived(at_x, at_y, at_z, at_core, part, valid=None):
        slot = slot_of(at_x, at_y, at_z, at_core)

        def take():
            pltpu.make_async_remote_copy(
                src_ref=part_of(slot, part), dst_ref=part_of(slot, part), send_sem=send_sem.at[0, 0, 0],
                recv_sem=recv_sem.at[part, slot], device_id=target[C], device_id_type=MESH,
            ).wait_recv()

        when(valid, take)

    def cross(at_z, part, valid):
        arrived(1 - x, y, at_z, core, part, valid)
        if part % 2 == 0:
            send(Y, (1 - x, y, at_z), part, valid)
        send(C, (1 - x, y, at_z), part, valid)
        arrived(x, 1 - y, at_z, core, part, valid)
        if part % 2 == 1:
            send(X, (x, 1 - y, at_z), part, valid)
        send(C, (x, 1 - y, at_z), part, valid)

    def corner(at_z, part, valid):
        arrived(1 - x, 1 - y, at_z, core, part, valid)
        send(C, (1 - x, 1 - y, at_z), part, valid)

    def level(far):
        if far == 0:
            return [(z, None)]
        return [(z - far, z >= far), (z + far, z + far < depth)]

    def begin(part):
        send(UP, (x, y, z), part, z < depth - 1, True)
        send(DOWN, (x, y, z), part, z > 0, True)
        for way in (X, Y, C):
            send(way, (x, y, z), part, None, True)

    def carry(parts):
        for far in range(1, depth + CORNER_LAG):
            if far < depth:
                for part in parts:
                    for (at_z, valid), way, onward in zip(level(far), (UP, DOWN), (z < depth - 1, z > 0)):
                        arrived(x, y, at_z, core, part, valid)
                        send(way, (x, y, at_z), part, valid & onward)
                        for side in (X, Y, C):
                            send(side, (x, y, at_z), part, valid)
            if 0 <= far - CROSS_LAG < depth:
                for part in parts:
                    for at_z, valid in level(far - CROSS_LAG):
                        cross(at_z, part, valid)
            if 0 <= far - CORNER_LAG < depth:
                for part in parts:
                    for at_z, valid in level(far - CORNER_LAG):
                        corner(at_z, part, valid)

    def collect(parts):
        for part in parts:
            for at_z in range(depth):
                for at_y in range(SIDE):
                    for at_x in range(SIDE):
                        arrived(at_x, at_y, at_z, 1 - core, part)

    values = range(1, PARTS + 1)
    begin(0)
    for part in values:
        begin(part)
    carry([0, *values])
    collect([0])

    wanted_row, wanted_col = meta_ref[ROWS : ROWS + 1], meta_ref[ROWS + 1 : ROWS + 2]
    lane = lax.broadcasted_iota(jnp.int32, (ROWS, LANES), 1)
    before = (
        lax.broadcasted_iota(jnp.int32, (LANES, LANES), 0) < lax.broadcasted_iota(jnp.int32, (LANES, LANES), 1)
    ).astype(jnp.float32)
    for at_z in range(depth):
        none = jnp.full((ROWS, LANES), -1, jnp.int32)
        slot_row, slot_col = none, none
        for t in range(terms):
            ids = ids_ref[at_z * terms + t]
            slot_row = jnp.where(ids == wanted_row, t, slot_row)
            slot_col = jnp.where(ids == wanted_col, t, slot_col)
        present = (slot_row >= 0) & (slot_col >= 0)
        code = (lane * terms + slot_row) * terms + slot_col
        ones = jnp.where(present, 1.0, 0.0).astype(jnp.float32)
        ahead = jnp.dot(ones, before, preferred_element_type=jnp.float32)
        place = jnp.where(present, ahead, float(LANES)).astype(jnp.int32)
        count = jnp.sum(jnp.where(present, 1, 0), axis=1, keepdims=True)
        entries = jnp.where(lane == LANES - 1, count, jnp.where(lane >= count, blocks * terms * terms, 0))
        for b in range(blocks):
            entries = entries + jnp.where(place[:, b : b + 1] == lane, code[:, b : b + 1], 0)
        list_ref[at_z * ROWS : (at_z + 1) * ROWS] = entries

    collect(values)
    own.wait()
    for way, place, part, valid, first in sent:
        when(valid, lambda: copy(way, place, part, first).wait_send())


def gather_by_hand(meta, shard, depth, blocks):
    terms = CORES * SIDE * SIDE
    slots = depth * terms
    return pl.pallas_call(
        functools.partial(gather_kernel, depth, blocks),
        out_shape=(
            jax.ShapeDtypeStruct((slots,) + shard.shape, shard.dtype),
            jax.ShapeDtypeStruct((depth * ROWS, LANES), jnp.int32),
        ),
        in_specs=[pl.BlockSpec(memory_space=pltpu.VMEM), pl.BlockSpec(memory_space=pl.ANY)],
        out_specs=(pl.BlockSpec(memory_space=pl.ANY), pl.BlockSpec(memory_space=pltpu.VMEM)),
        scratch_shapes=[
            pltpu.VMEM((slots, ROWS, LANES), jnp.int32),
            pltpu.SemaphoreType.DMA,
            pltpu.SemaphoreType.DMA((1 + PARTS, 5, depth * SIDE * SIDE)),
            pltpu.SemaphoreType.DMA((1 + PARTS, slots)),
        ],
        compiler_params=pltpu.CompilerParams(collective_id=0, has_side_effects=True),
    )(meta, shard)


def split(value):
    high = value.astype(jnp.bfloat16)
    return high, (value - high.astype(jnp.float32)).astype(jnp.bfloat16)


def prepare(value, s, left_ref, right_ref):
    size = value.shape[0]
    high, low = split(value)
    right_ref[s, :size] = high
    right_ref[s, size : 2 * size] = high
    right_ref[s, 2 * size :] = low
    high, low = split(value.T)
    left_ref[s, :, :size] = high
    left_ref[s, :, size : 2 * size] = low
    left_ref[s, :, 2 * size :] = high


def add_products(slots, read, count, out_ref, left_ref, right_ref, filled):
    def entries(first, width):
        picked = []
        for k in range(width):
            code = read(first + k)
            pair = code % (slots * slots)
            picked.append((code // (slots * slots), pair // slots, pair % slots))
        sums = [
            out_ref[b] + jnp.dot(left_ref[r], right_ref[c], preferred_element_type=jnp.float32)
            for b, r, c in picked
        ]
        for (b, _, _), value in zip(picked, sums):
            out_ref[b] = value

    groups = (count + UNROLL - 1) // UNROLL if filled else count // UNROLL
    pl.loop(0, groups)(lambda i: entries(i * UNROLL, UNROLL))
    if filled:
        return
    pl.loop(groups * UNROLL, count)(lambda i: entries(i, 1))


def clear(out_ref):
    def one(b, _):
        out_ref[b] = jnp.zeros(out_ref.shape[1:], jnp.float32)
        return 0

    lax.fori_loop(0, out_ref.shape[0], one, 0)


def held_kernel(terms, panels_each, list_ref, tiles_ref, out_ref, held_ref, total_ref, left_ref, right_ref, in_sem, out_sem):
    slots = tiles_ref.shape[0]
    size = tiles_ref.shape[2]

    def fetch(slot):
        return pltpu.make_async_copy(tiles_ref.at[slot], held_ref.at[slot], in_sem.at[slot])

    for slot in range(slots):
        fetch(slot).start()
    clear(total_ref)

    def panel(group, j):
        row = pl.multiple_of(j * size, size)
        for s in range(terms):
            prepare(held_ref[group * terms + s, pl.ds(row, size)], s, left_ref, right_ref)
        add_products(
            terms, lambda k: list_ref[group * ROWS + j, k], list_ref[group * ROWS + j, LANES - 1],
            total_ref, left_ref, right_ref, True,
        )

    def of_group(group):
        for s in range(terms):
            fetch(group * terms + s).wait()
        pl.loop(0, panels_each)(lambda j: panel(group, j))

    pl.loop(0, slots // terms)(of_group)
    pieces = out_sem.shape[0]
    each = out_ref.shape[0] // pieces
    outs = [
        pltpu.make_async_copy(total_ref.at[pl.ds(i * each, each)], out_ref.at[pl.ds(i * each, each)], out_sem.at[i])
        for i in range(pieces)
    ]
    for out in outs:
        out.start()
    for out in outs:
        out.wait()


def held_products(tiles, entries, terms, panels_each, blocks):
    slots, _, size = tiles.shape
    pieces = next(n for n in (8, 7, 4, 2, 1) if blocks % n == 0)
    return pl.pallas_call(
        functools.partial(held_kernel, terms, panels_each),
        out_shape=jax.ShapeDtypeStruct((blocks, size, size), jnp.float32),
        in_specs=[pl.BlockSpec(memory_space=pltpu.SMEM), pl.BlockSpec(memory_space=pl.ANY)],
        out_specs=pl.BlockSpec(memory_space=pl.ANY),
        scratch_shapes=[
            pltpu.VMEM(tiles.shape, jnp.float32),
            pltpu.VMEM((blocks + 1, size, size), jnp.float32),
            pltpu.VMEM((terms, size, 3 * size), jnp.bfloat16),
            pltpu.VMEM((terms, 3 * size, size), jnp.bfloat16),
            pltpu.SemaphoreType.DMA((slots,)),
            pltpu.SemaphoreType.DMA((pieces,)),
        ],
        compiler_params=pltpu.CompilerParams(vmem_limit_bytes=56 * 1024 * 1024),
    )(entries, tiles)


def product_kernel(slots, base, count_ref, list_ref, tiles_ref, out_ref, left_ref, right_ref):
    panel = pl.program_id(0)

    pl.when(panel == 0)(lambda: clear(out_ref))
    pl.loop(0, slots)(lambda s: prepare(tiles_ref[0, s], s, left_ref, right_ref))
    add_products(
        slots, lambda k: list_ref[panel * base + k], count_ref[panel], out_ref, left_ref, right_ref, False
    )


def products(tiles, slots, panels_each, counts, entries, blocks):
    groups, size = tiles.shape[0], tiles.shape[3]
    return pl.pallas_call(
        functools.partial(product_kernel, slots, entries.shape[1]),
        out_shape=jax.ShapeDtypeStruct((blocks, size, size), jnp.float32),
        grid_spec=pltpu.PrefetchScalarGridSpec(
            num_scalar_prefetch=2,
            grid=(groups * panels_each,),
            in_specs=[
                pl.BlockSpec(
                    (1, slots, size, size), lambda p, *_: (p // panels_each, 0, p % panels_each, 0)
                )
            ],
            out_specs=pl.BlockSpec((blocks, size, size), lambda p, *_: (0, 0, 0)),
            scratch_shapes=[
                pltpu.VMEM((slots, size, 3 * size), jnp.bfloat16),
                pltpu.VMEM((slots, 3 * size, size), jnp.bfloat16),
            ],
        ),
        compiler_params=pltpu.CompilerParams(
            dimension_semantics=("arbitrary",), vmem_limit_bytes=56 * 1024 * 1024
        ),
    )(counts, entries.reshape(-1), tiles)


def block_list(ids, rows, cols):
    slots, blocks = ids.shape[1], rows.shape[0]
    order = jnp.arange(slots, dtype=jnp.int32)[None, :, None]
    match_row = ids[:, :, None] == rows[None, None, :]
    match_col = ids[:, :, None] == cols[None, None, :]
    slot_row = jnp.sum(jnp.where(match_row, order, 0), axis=1)
    slot_col = jnp.sum(jnp.where(match_col, order, 0), axis=1)
    present = jnp.any(match_row, axis=1) & jnp.any(match_col, axis=1)
    number = jnp.arange(blocks, dtype=jnp.int32)
    code = (number[None, :] * slots + slot_row) * slots + slot_col
    ahead = jnp.sum(
        jnp.where(present[:, None, :] & (number[None, None, :] < number[None, :, None]), 1, 0), axis=2
    )
    chosen = present[:, None, :] & (ahead[:, None, :] == number[None, :, None])
    entries = jnp.sum(jnp.where(chosen, code[:, None, :], 0), axis=2)
    counts = jnp.sum(present.astype(jnp.int32), axis=1)
    return counts.astype(jnp.int32), entries.astype(jnp.int32)


def solution(mesh):
    depth, terms = mesh.shape["rep"], mesh.shape["term"]

    def by_hand(panel_values, panel_ids, rows, cols, blocks):
        panels_each, _, passages, size = panel_values.shape
        ids = jnp.broadcast_to(panel_ids, (panels_each, LANES))
        ids = jnp.pad(ids, ((0, ROWS - panels_each), (0, 0)), constant_values=-1)
        here = lax.axis_index("rep") == jnp.arange(depth, dtype=jnp.int32)
        both = jnp.stack([rows, cols]).reshape(2, depth, blocks)
        both = jnp.sum(jnp.where(here[None, :, None], both, 0), axis=1)
        both = jnp.pad(both, ((0, ROWS - 2), (0, LANES - blocks)), constant_values=-2)
        tiles, entries = gather_by_hand(
            jnp.concatenate([ids, both]), panel_values.reshape(panels_each * passages, size), depth, blocks
        )
        return held_products(tiles, entries, terms, panels_each, blocks)

    def local(panel_values, panel_ids, block_rows, block_cols):
        panels_each, own_slots, passages, size = panel_values.shape
        blocks = block_rows.shape[0] // depth
        slots = terms * own_slots
        if terms == CORES * SIDE * SIDE and own_slots == 1 and panels_each <= ROWS and blocks + UNROLL < LANES:
            return by_hand(panel_values, panel_ids, block_rows, block_cols, blocks)
        first = lax.axis_index("rep") * blocks
        rows = lax.dynamic_slice_in_dim(block_rows, first, blocks)
        cols = lax.dynamic_slice_in_dim(block_cols, first, blocks)
        shard = jnp.swapaxes(panel_values, 0, 1).reshape(own_slots, panels_each * passages, size)
        tiles = lax.all_gather(shard, ("rep", "term"), axis=0, tiled=True)
        tiles = tiles.reshape(depth, slots, panels_each * passages, size)
        ids = lax.all_gather(panel_ids.T, ("rep", "term"), axis=0, tiled=True)
        ids = ids.reshape(depth, slots, panels_each)
        ids = jnp.swapaxes(ids, 1, 2).reshape(depth * panels_each, slots)
        counts, entries = block_list(ids, rows, cols)
        return products(tiles, slots, panels_each, counts, entries, blocks)

    placed = (P("rep", "term", None, None), P("rep", "term"), P("term"), P("term"))
    return jax.shard_map(
        local, mesh=mesh, in_specs=placed, out_specs=P(("term", "rep"), None, None), check_vma=False
    )
```
